32 devices in a mesh: dp: 16 (over z, x, core), ep: 2 (over y).
Axes of the slice: x: 2, y: 2, z: 4, core: 2. Of those that a mesh axis runs over, the one named last changes fastest.
Arguments:
- query_rows: bfloat16 [32, 128, 576], P(('dp', 'ep')), may hold values from -65 to 65, as said below
- cache_latent: bfloat16 [131072, 576], P(('dp', 'ep')), may hold values from -6 to 6, as said below
- lengths: int32 [32], replicated, may hold values from 2 to 4096, as said below
- moe_input: bfloat16 [256, 7168], P(('dp', 'ep')), may hold values from -6 to 6
- expert_ids: int32 [256, 8], P(('dp', 'ep')), may hold values from 0 to 15, all different within a row; in each aligned block of 8 rows (0 to 7, 8 to 15, ...) at most 4 rows name the same one
- gate_weights: float32 [256, 8], P(('dp', 'ep')), may hold values from 0.05 to 0.5
- expert_gate: bfloat16 [16, 7168, 1024], P('dp', None, 'ep'), may hold values from -0.0625 to 0.0625
- expert_up: bfloat16 [16, 7168, 1024], P('dp', None, 'ep'), may hold values from -0.0625 to 0.0625
- expert_down: bfloat16 [16, 1024, 7168], P('dp', 'ep'), may hold values from -0.1875 to 0.1875
Outputs:
- attn_out: bfloat16 [32, 128, 512], P(('dp', 'ep'))
- moe_out: bfloat16 [256, 7168], P(('dp', 'ep'))
The draws below stay inside these ranges and needn't reach their ends.
Inputs may be any that keep to these rules, and one draw needn't show every extreme that they name: `lengths`: some request has exactly 4096 cached tokens in every draw. `expert_ids`: each row names 8 different experts. Among the rows of one device no expert is named more than 4 times, a bound that some block reaches. `cache_latent`: finite latent entries. `query_rows`: finite query entries.
All inputs are finite; a program needn't handle non-finite values.
Results may differ from the reference program's by a relative error of at most 0.008.
Values may be sent and summed in bfloat16 or wider, within the bound.
A program may use at most 128 MiB of HBM per device.

```python
import math
import jax
import jax.numpy as jnp
import numpy as np
from jax import lax

WIDTH = 7168
HEADS = 128
LATENT = 512
KEY_DIM = 576
EXPERT_HIDDEN = 1024
TOPK = 8
EXPERTS = 16
MOE_TOK = 8
CAPACITY = 4
CTX_TOK = 4096
REQUESTS = 32
MOE_TOKENS = 256
N_EP = 2


def joint_plan(key):
    base_key = jax.random.fold_in(key, 4242)
    keys_all = jax.random.split(base_key, 3)
    first = jax.random.randint(keys_all[0], (REQUESTS,), 0, CTX_TOK)
    second = jax.random.randint(keys_all[1], (REQUESTS,), 0, CTX_TOK)
    raw_lengths = first * second // CTX_TOK + 2
    chosen = jax.random.randint(keys_all[2], (), 0, REQUESTS)
    lengths = jnp.where(jnp.arange(REQUESTS, dtype=jnp.int32) == chosen, CTX_TOK, raw_lengths).astype(jnp.int32)
    return lengths


def draw_lengths(key, part):
    return joint_plan(key)


def draw_cache_latent(key, part):
    noise_key = jax.random.fold_in(key, 77)
    values = jnp.clip(jax.random.normal(noise_key, (REQUESTS, CTX_TOK, KEY_DIM), jnp.float32), -6.0, 6.0)
    return values.reshape(REQUESTS * CTX_TOK, KEY_DIM).astype(jnp.bfloat16)


def draw_query_rows(key, part):
    noise_key = jax.random.fold_in(key, 91)
    values = jnp.clip(jax.random.normal(noise_key, (REQUESTS, HEADS, KEY_DIM), jnp.float32), -6.0, 6.0)
    return values.astype(jnp.bfloat16)


def block_levels(own_key, dims, cuts, low, top_value):
    factor_of, own = 1.0, jax.random.fold_in(own_key, 6)
    for dim, blocks in cuts:
        heights = jnp.exp(jax.random.uniform(jax.random.fold_in(own, dim), (blocks,), jnp.float32, low / len(cuts), top_value / len(cuts)))
        factor_of = factor_of * jnp.repeat(heights, dims[dim] // blocks).reshape([-1 if axis == dim else 1 for axis in range(len(dims))])
    return factor_of


def deal_out(key, own, number, rows, number_of, top, limit, slope):
    sequence = jax.random.permutation(key, number_of)
    packed, usual = shares(number_of, rows * top, limit, slope, True), shares(number_of, rows * top, limit, slope, False)
    places = jnp.arange(number_of)

    def named(sizes, offset_by):
        used = int((sizes > 0).sum())
        fixed = max(1, used // 4)
        passed = fixed + (places - fixed + offset_by * (used - fixed)) % max(1, number_of - fixed)
        return jnp.zeros((number_of,), jnp.int32).at[sequence[jnp.where(places < fixed, places, passed)]].set(jnp.asarray(sizes, jnp.int32))

    sizes = jnp.where(number % 4 == 0, named(packed, number // 4), named(usual, number - number // 4 - 1))
    mixed = jax.random.permutation(jax.random.fold_in(own, 3), number_of)
    source_of, sink = mixed[0:number_of // 2 * 2:2], mixed[1:number_of // 2 * 2:2]
    room = jnp.minimum(sizes[source_of] - 1, limit - sizes[sink]) // 2
    room = jnp.where((source_of == sequence[0]) | (sink == sequence[0]) | (sizes[sink] == 0), 0, jnp.maximum(room, 0))
    passed = jax.random.randint(jax.random.fold_in(own, 4), (number_of // 2,), 0, 1 << 20) % (room + 1)
    sizes = sizes.at[source_of].add(-passed).at[sink].add(passed)
    labels = jnp.searchsorted(jnp.cumsum(sizes), jnp.arange(rows * top), side="right").astype(jnp.int32)
    listing = labels.reshape(top, rows).T
    listing = listing[jax.random.permutation(jax.random.fold_in(own, 1), rows)]
    offset_by = jax.random.randint(jax.random.fold_in(own, 2), (rows, 1), 0, top)
    return jnp.take_along_axis(listing, (jnp.arange(top)[None, :] + offset_by) % top, axis=1)


def shares(number_of, total, limit, skew, full):
    portions = [(1 << 20) // math.isqrt(standing ** skew) + 1 for standing in range(1, number_of + 1)]
    largest = limit if full else min(limit, max(-(-total // number_of), total * portions[0] // sum(portions)))
    least = 1 if total - largest >= number_of - 1 else 0
    holding, rest = [largest] + [least] * (number_of - 1), total - largest - least * (number_of - 1)
    while rest > 0:
        candidates = [i for i in range(1, number_of) if holding[i] < largest] or [i for i in range(1, number_of) if holding[i] < limit]
        pool, budget = sum([portions[i] for i in candidates]), rest
        for i in candidates:
            addition = min(limit - holding[i], max(1, budget * portions[i] // pool), rest)
            holding[i] = holding[i] + addition
            rest = rest - addition
    return np.array(holding)


def bell_draw(key, extent, spread, limit, shards=(), kind=jnp.bfloat16):
    array = spread * jax.random.normal(key, extent, jnp.float32)
    if shards:
        array = array * block_levels(key, extent, shards, -0.22, 0.18)
    return jnp.clip(array, -limit, limit).astype(kind)


def setup_inputs(seed: int = 0) -> dict:
    key_of = jax.random.split(jax.random.key(seed), 10)
    query_rows = draw_query_rows(jax.random.fold_in(key_of[9], 71), 0)
    cache_latent = draw_cache_latent(jax.random.fold_in(key_of[9], 71), 0)
    lengths = draw_lengths(jax.random.fold_in(key_of[9], 71), 0)
    moe_input = bell_draw(key_of[3], (MOE_TOKENS, WIDTH), 1.0, 6.0, ((0, 32),))
    expert_ids_keys = jax.random.split(jax.random.fold_in(key_of[4], 1), MOE_TOKENS // MOE_TOK)
    expert_ids_turns = jax.random.permutation(jax.random.fold_in(key_of[4], 3), MOE_TOKENS // MOE_TOK)
    expert_ids = jax.vmap(lambda own, number: deal_out(jax.random.fold_in(key_of[4], 2), own, number, MOE_TOK, EXPERTS, TOPK, CAPACITY, 2))(expert_ids_keys, expert_ids_turns).reshape((MOE_TOKENS, TOPK))
    gate_weights = jnp.clip(jnp.exp(math.log(0.5) - 2.3025851 * jax.random.uniform(key_of[5], (MOE_TOKENS, TOPK), jnp.float32) ** block_levels(key_of[5], (MOE_TOKENS, TOPK), ((0, 32),), -0.2, 0.2)), 0.05, 0.5)
    expert_gate = bell_draw(key_of[6], (EXPERTS, WIDTH, EXPERT_HIDDEN), WIDTH ** -0.5, 0.0625, ((0, 16), (2, 2)))
    expert_up = bell_draw(key_of[7], (EXPERTS, WIDTH, EXPERT_HIDDEN), WIDTH ** -0.5, 0.0625, ((0, 16), (2, 2)))
    expert_down = bell_draw(key_of[8], (EXPERTS, EXPERT_HIDDEN, WIDTH), EXPERT_HIDDEN ** -0.5, 0.1875, ((0, 16), (1, 2)))
    return {"query_rows": query_rows, "cache_latent": cache_latent, "lengths": lengths, "moe_input": moe_input, "expert_ids": expert_ids, "gate_weights": gate_weights, "expert_gate": expert_gate, "expert_up": expert_up, "expert_down": expert_down}


qk_scale = 192.0 ** -0.5


def attend_one(inputs):
    query_row, cache_rows, seq_length = inputs
    scores = qk_scale * jnp.dot(query_row, cache_rows.T, preferred_element_type=jnp.float32)
    live_mask = jnp.arange(CTX_TOK, dtype=jnp.int32)[None, :] < seq_length
    scores = jnp.where(live_mask, scores, -1e30)
    score_top = jnp.max(scores, axis=1, keepdims=True)
    exponent = jnp.where(live_mask, jnp.exp(scores - score_top), 0.0)
    weight_sum = jnp.sum(exponent, axis=1, keepdims=True)
    mixed_values = jnp.dot(exponent.astype(jnp.bfloat16), cache_rows[:, :LATENT], preferred_element_type=jnp.float32)
    return (mixed_values / weight_sum).astype(jnp.bfloat16)


def expert_rows(row_block, gate_proj, up_proj, down_proj):
    gate_act = jnp.dot(row_block, gate_proj, preferred_element_type=jnp.float32)
    up_act = jnp.dot(row_block, up_proj, preferred_element_type=jnp.float32)
    hidden = (jax.nn.silu(gate_act) * up_act).astype(jnp.bfloat16)
    group_size = EXPERT_HIDDEN // N_EP
    running_sum = jnp.zeros((row_block.shape[0], WIDTH), jnp.float32)
    for group_number in range(N_EP):
        lower = group_number * group_size
        partial_sum = jnp.dot(hidden[:, lower:lower + group_size], down_proj[lower:lower + group_size], preferred_element_type=jnp.float32)
        rounded = lax.optimization_barrier(partial_sum.astype(jnp.bfloat16))
        running_sum = running_sum + rounded.astype(jnp.float32)
    return running_sum.astype(jnp.bfloat16)


def reference(query_rows, cache_latent, lengths, moe_input, expert_ids, gate_weights, expert_gate, expert_up, expert_down):
    attn_out = lax.map(attend_one, (query_rows, cache_latent.reshape(REQUESTS, CTX_TOK, KEY_DIM), lengths))
    source_count = MOE_TOKENS // MOE_TOK
    slot_count = MOE_TOK * TOPK
    flat_ids = expert_ids.reshape(source_count, slot_count)
    onehot = (flat_ids[:, :, None] == jnp.arange(EXPERTS, dtype=jnp.int32)[None, None, :]).astype(jnp.int32)
    before = jnp.cumsum(onehot, axis=1) - onehot
    position = jnp.sum(before * onehot, axis=2).astype(jnp.int32)
    source_index = jnp.broadcast_to(jnp.arange(source_count, dtype=jnp.int32)[:, None], (source_count, slot_count))
    token_index = source_index * MOE_TOK + jnp.arange(slot_count, dtype=jnp.int32)[None, :] // TOPK
    table = jnp.full((source_count, EXPERTS, CAPACITY), MOE_TOKENS, dtype=jnp.int32)
    table = table.at[source_index, flat_ids, position].set(token_index)
    padded = jnp.concatenate([moe_input, jnp.zeros((1, WIDTH), moe_input.dtype)], axis=0)

    def one_expert(inputs):
        expert_table, gate_proj, up_proj, down_proj = inputs
        row_block = padded[expert_table.reshape(-1)]
        return expert_rows(row_block, gate_proj, up_proj, down_proj).reshape(source_count, CAPACITY, WIDTH)

    expert_out = lax.map(one_expert, (jnp.transpose(table, (1, 0, 2)), expert_gate, expert_up, expert_down))
    token_pos = position.reshape(MOE_TOKENS, TOPK)
    token_src = jnp.arange(MOE_TOKENS, dtype=jnp.int32) // MOE_TOK
    running_sum = jnp.zeros((MOE_TOKENS, WIDTH), jnp.float32)
    for slot_number in range(TOPK):
        picked = expert_out[expert_ids[:, slot_number], token_src, token_pos[:, slot_number]]
        running_sum = running_sum + gate_weights[:, slot_number:slot_number + 1] * picked.astype(jnp.float32)
    return attn_out, running_sum.astype(jnp.bfloat16)
```

```python
import jax
import jax.numpy as jnp
from jax import lax
from jax.sharding import PartitionSpec as P

WIDTH = 7168
LATENT = 512
TOPK = 8


qk_scale = 192.0 ** (-0.5)
far_low = -1e30
attend_rows = 512


def partial_attend(query_row, key_rows, live_mask):
    scores = qk_scale * lax.dot_general(
        query_row, key_rows, (((1,), (1,)), ((), ())), preferred_element_type=jnp.float32
    )
    scores = jnp.where(live_mask[None, :], scores, far_low)
    score_top = jnp.max(scores, axis=1)
    exponent = jnp.where(live_mask[None, :], jnp.exp(scores - score_top[:, None]), 0.0)
    weight_sum = jnp.sum(exponent, axis=1)
    mixed_values = jnp.dot(
        exponent.astype(jnp.bfloat16), key_rows[:, :LATENT], preferred_element_type=jnp.float32
    )
    return (score_top, weight_sum, mixed_values)


def merge_parts(first, second):
    top_first, sum_first, mix_first = first
    top_second, sum_second, mix_second = second
    score_top = jnp.maximum(top_first, top_second)
    scale_first = jnp.exp(top_first - score_top)
    scale_second = jnp.exp(top_second - score_top)
    return (
        score_top,
        sum_first * scale_first + sum_second * scale_second,
        mix_first * scale_first[:, None] + mix_second * scale_second[:, None],
    )


def local_attend(query_row, cache_rows, keep_end):
    head_count = query_row.shape[0]
    block_total = (keep_end + attend_rows - 1) // attend_rows
    initial = (
        jnp.full((head_count,), far_low, jnp.float32),
        jnp.zeros((head_count,), jnp.float32),
        jnp.zeros((head_count, LATENT), jnp.float32),
    )

    def block_step(block_index, carry):
        start_row = block_index * attend_rows
        key_rows = lax.dynamic_slice_in_dim(cache_rows, start_row, attend_rows, 0)
        live_mask = start_row + jnp.arange(attend_rows, dtype=jnp.int32) < keep_end
        return merge_parts(carry, partial_attend(query_row, key_rows, live_mask))

    return lax.fori_loop(0, block_total, block_step, initial)


def per_device(
    query_rows,
    cache_latent,
    lengths,
    moe_input,
    expert_ids,
    gate_weights,
    expert_gate,
    expert_up,
    expert_down,
):
    ranks_dp = lax.axis_size("dp")
    ranks_ep = lax.axis_size("ep")
    here_dp = lax.axis_index("dp")
    here_ep = lax.axis_index("ep")
    own_rank = here_dp * ranks_ep + here_ep
    own_length = lengths[own_rank]
    query_row = query_rows[0]
    score_top, weight_sum, mixed_values = local_attend(query_row, cache_latent, own_length)
    attn_out = (mixed_values / weight_sum[:, None]).astype(jnp.bfloat16)[None]
    axes = ("dp", "ep")
    all_rows = lax.all_gather(moe_input, axes, axis=0, tiled=True)
    all_ids = lax.all_gather(expert_ids, axes, axis=0, tiled=True)
    all_weights = lax.all_gather(gate_weights, axes, axis=0, tiled=True)
    row_weight = jnp.sum(jnp.where(all_ids == here_dp, all_weights, 0.0), axis=1, keepdims=True)
    gate_act = jnp.dot(all_rows, expert_gate[0], preferred_element_type=jnp.float32)
    up_act = jnp.dot(all_rows, expert_up[0], preferred_element_type=jnp.float32)
    hidden = (jax.nn.silu(gate_act) * up_act).astype(jnp.bfloat16)
    partial_sum = jnp.dot(hidden, expert_down[0], preferred_element_type=jnp.float32)
    weighted = (partial_sum * row_weight).astype(jnp.bfloat16)
    moe_sum = lax.psum_scatter(weighted, axes, scatter_dimension=0, tiled=True)
    return (attn_out, moe_sum.astype(jnp.bfloat16))


def solution(mesh):
    placed = (
        P(("dp", "ep"), None, None),
        P(("dp", "ep"), None),
        P(),
        P(("dp", "ep"), None),
        P(("dp", "ep"), None),
        P(("dp", "ep"), None),
        P("dp", None, "ep"),
        P("dp", None, "ep"),
        P("dp", "ep", None),
    )
    return jax.shard_map(
        per_device,
        mesh=mesh,
        in_specs=placed,
        out_specs=(P(("dp", "ep"), None, None), P(("dp", "ep"), None)),
        check_vma=False,
    )
```

```python
import functools

import jax
import jax.numpy as jnp
from jax import lax
from jax.experimental import pallas as pl
from jax.experimental.pallas import tpu as pltpu
from jax.sharding import PartitionSpec as P

WIDTH = 7168
LATENT = 512
TOPK = 8


qk_scale = 192.0 ** (-0.5)
far_low = -1e30
attend_rows = 512


def partial_attend(query_row, key_rows, live_mask):
    scores = qk_scale * lax.dot_general(
        query_row, key_rows, (((1,), (1,)), ((), ())), preferred_element_type=jnp.float32
    )
    scores = jnp.where(live_mask[None, :], scores, far_low)
    score_top = jnp.max(scores, axis=1)
    exponent = jnp.where(live_mask[None, :], jnp.exp(scores - score_top[:, None]), 0.0)
    weight_sum = jnp.sum(exponent, axis=1)
    mixed_values = jnp.dot(
        exponent.astype(jnp.bfloat16), key_rows[:, :LATENT], preferred_element_type=jnp.float32
    )
    return (score_top, weight_sum, mixed_values)


def merge_parts(first, second):
    top_first, sum_first, mix_first = first
    top_second, sum_second, mix_second = second
    score_top = jnp.maximum(top_first, top_second)
    scale_first = jnp.exp(top_first - score_top)
    scale_second = jnp.exp(top_second - score_top)
    return (
        score_top,
        sum_first * scale_first + sum_second * scale_second,
        mix_first * scale_first[:, None] + mix_second * scale_second[:, None],
    )


def local_attend(query_row, cache_rows, keep_end):
    head_count = query_row.shape[0]
    block_total = (keep_end + attend_rows - 1) // attend_rows
    initial = (
        jnp.full((head_count,), far_low, jnp.float32),
        jnp.zeros((head_count,), jnp.float32),
        jnp.zeros((head_count, LATENT), jnp.float32),
    )

    def block_step(block_index, carry):
        start_row = block_index * attend_rows
        key_rows = lax.dynamic_slice_in_dim(cache_rows, start_row, attend_rows, 0)
        live_mask = start_row + jnp.arange(attend_rows, dtype=jnp.int32) < keep_end
        return merge_parts(carry, partial_attend(query_row, key_rows, live_mask))

    return lax.fori_loop(0, block_total, block_step, initial)


def expert_kernel(
    dims, expert_total, x_ref, gate_hbm, up_hbm, down_hbm, out_ref,
    rows_in, rows_out, gate_buf, up_buf, down_buf, act_buf, weight_buf,
    core_in, first_in, second_in, plane_in,
    load_sem, z_sem, near_sem, far_sem, core_sem, rcore_sem, rfirst_sem, rsecond_sem, rplane_sem,
):
    nz, nx, ny = dims
    width = down_buf.shape[1]
    half = width // 2
    full = rows_in.shape[2]
    dp, y = lax.axis_index("dp"), lax.axis_index("ep")
    core, x, z = dp % 2, (dp // 2) % nx, dp // (2 * nx)

    def slot(k, a, b, other=0):
        c = 1 - core if other else core
        return ((((z + k) % nz) * nx + (x + a) % nx) * 2 + c) * ny + (y + b) % ny

    def device(k=0, a=0, b=0, other=0):
        c = 1 - core if other else core
        return ((((z + k) % nz) * nx + (x + a) % nx) * 2 + c, (y + b) % ny)

    def span(h, top):
        return pl.ds(0, half) if h == 0 else pl.ds(half, top - half)

    loads = [
        pltpu.make_async_copy(gate_hbm.at[0], gate_buf, load_sem.at[1]),
        pltpu.make_async_copy(up_hbm.at[0], up_buf, load_sem.at[2]),
        pltpu.make_async_copy(down_hbm.at[0], down_buf, load_sem.at[3]),
    ]
    mine = pltpu.make_async_copy(x_ref, rows_in.at[slot(0, 0, 0)], load_sem.at[0])
    mine.start()
    barrier = pltpu.get_barrier_semaphore()
    partners = [device(other=1)]
    partners += [device(k=k) for k in range(1, nz)]
    partners += [device(a=a) for a in range(1, nx)]
    partners += [device(b=b) for b in range(1, ny)]
    for partner in partners:
        pl.semaphore_signal(barrier, inc=1, device_id=partner, device_id_type=pl.DeviceIdType.MESH)
    for load in loads:
        load.start()
    pl.semaphore_wait(barrier, len(partners))
    mine.wait()

    def remote(src, dst, sems, index, target):
        return pltpu.make_async_remote_copy(
            src_ref=src,
            dst_ref=dst,
            send_sem=sems.at[(0,) + index],
            recv_sem=sems.at[(1,) + index],
            device_id=target,
            device_id_type=pl.DeviceIdType.MESH,
        )

    sent = []

    def send(copy):
        copy.start()
        sent.append(copy)

    def block_copy(source, h, sems, index, target):
        part = rows_in.at[source, :, span(h, full)]
        return remote(part, part, sems, index, target)

    def to_core(k, a, b, h):
        send(block_copy(slot(-k, -a, -b), h, core_sem, (k, a, b, h), device(other=1)))

    for h in range(2):
        for k in range(nz - 1, 0, -1):
            send(block_copy(slot(0, 0, 0), h, z_sem, (k, h), device(k=k)))

    axes = {0: (nx, ny), 1: (ny, nx)}

    def turn(h, first, second):
        return (first, second) if h == 0 else (second, first)

    def near(k, h, way, hop):
        a, b = turn(h, hop, 0) if way == 0 else turn(h, 0, hop)
        return block_copy(slot(-k, 0, 0), h, near_sem, (k, h, way, hop), device(a=a, b=b))

    def far(k, h, i, hop):
        a, b = turn(h, 0, hop)
        sa, sb = turn(h, i, 0)
        return block_copy(slot(-k, -sa, -sb), h, far_sem, (k, h, i, hop), device(a=a, b=b))

    def stage_a(k):
        for h in range(2):
            if k > 0:
                block_copy(slot(-k, 0, 0), h, z_sem, (k, h), device(k=k)).wait_recv()
            for way in range(2):
                for hop in range(1, axes[h][way]):
                    send(near(k, h, way, hop))
            to_core(k, 0, 0, h)

    def arrived(k, a, b, h, sems, index):
        block_copy(slot(-k, -a, -b), h, sems, index, device(other=1)).wait_recv()

    def stage_b(k):
        for h in range(2):
            for i in range(1, axes[h][0]):
                a, b = turn(h, i, 0)
                arrived(k, a, b, h, near_sem, (k, h, 0, i))
                for hop in range(1, axes[h][1]):
                    send(far(k, h, i, hop))
                to_core(k, a, b, h)

    def stage_c(k):
        for h in range(2):
            for hop in range(1, axes[h][1]):
                a, b = turn(h, 0, hop)
                arrived(k, a, b, h, near_sem, (k, h, 1, hop))
                to_core(k, a, b, h)
                for i in range(1, axes[h][0]):
                    a, b = turn(h, i, hop)
                    arrived(k, a, b, h, far_sem, (k, h, i, hop))
                    to_core(k, a, b, h)

    for step in range(nz + 2):
        if step < nz:
            stage_a(step)
        if 0 <= step - 1 < nz:
            stage_b(step - 1)
        if 0 <= step - 2 < nz:
            stage_c(step - 2)
    for k in range(nz):
        for a in range(nx):
            for b in range(ny):
                for h in range(2):
                    block_copy(
                        slot(-k, -a, -b, 1), h, core_sem, (k, a, b, h), device(other=1)
                    ).wait_recv()
    loads[0].wait()
    loads[1].wait()
    count, rows = rows_in.shape[0], rows_in.shape[1]
    total = count * rows
    hidden_units = gate_buf.shape[1]
    depth = 1024
    act_buf[...] = jnp.zeros_like(act_buf)

    @pl.loop(0, width // depth)
    def _(step):
        cols = pl.ds(pl.multiple_of(step * depth, depth), depth)
        lhs = rows_in[:, :, cols].astype(jnp.float32).reshape(total, depth).astype(jnp.bfloat16)
        act_buf[0] += jnp.dot(lhs, gate_buf[cols, :], preferred_element_type=jnp.float32)
        act_buf[1] += jnp.dot(lhs, up_buf[cols, :], preferred_element_type=jnp.float32)

    coded = rows_in[:, :, width:].astype(jnp.float32).reshape(total, full - width)
    lane = lax.broadcasted_iota(jnp.int32, coded.shape, 1)
    chosen = (lane == dp) | (lane == dp + expert_total) | (lane == dp + 2 * expert_total)
    weight_buf[...] = jnp.sum(jnp.where(chosen, coded, 0.0), axis=1, keepdims=True)
    gate_act = act_buf[0]
    hidden = (gate_act / (1.0 + jnp.exp(-gate_act)) * act_buf[1]).astype(jnp.bfloat16)
    loads[2].wait()
    piece = 512
    for h in range(2):

        @pl.loop(0, half // piece)
        def _(step, h=h):
            cols = pl.ds(pl.multiple_of(h * half + step * piece, piece), piece)
            product = jnp.dot(hidden, down_buf[:, cols], preferred_element_type=jnp.float32)
            product = product * weight_buf[...]
            rows_out[:, :, cols] = product.reshape(count, rows, piece).astype(jnp.bfloat16)

        for k in list(range(1, nz)) + [0]:
            for a in range(nx):
                for b in range(ny):
                    send(
                        remote(
                            rows_out.at[slot(k, a, b, 1), :, span(h, width)],
                            core_in.at[(k * nx + a) * ny + b, :, span(h, width)],
                            rcore_sem,
                            (k, a, b, h),
                            device(other=1),
                        )
                    )

    def add_into(target, h, landed):
        value = rows_out[target, :, span(h, width)].astype(jnp.float32)
        for piece_ref in landed:
            value = value + piece_ref[...].astype(jnp.float32)
        rows_out[target, :, span(h, width)] = value.astype(jnp.bfloat16)

    most = max(nx, ny)

    def first_copy(k, h, i, hop):
        a, b = turn(h, i, hop)
        da, db = turn(h, 0, hop)
        return remote(
            rows_out.at[slot(k, a, b), :, span(h, width)],
            first_in.at[h, (k * most + i) * most + hop],
            rfirst_sem, (k, h, i, hop), device(a=da, b=db),
        )

    def second_copy(k, h, i):
        a, b = turn(h, i, 0)
        return remote(
            rows_out.at[slot(k, a, b), :, span(h, width)],
            second_in.at[h, k * most + i],
            rsecond_sem, (k, h, i), device(a=a, b=b),
        )

    def plane_copy(k, h):
        return remote(
            rows_out.at[slot(k, 0, 0), :, span(h, width)],
            plane_in.at[k, :, span(h, width)],
            rplane_sem, (k, h), device(k=k),
        )

    def back_a(k):
        for h in range(2):
            for hop in list(range(1, axes[h][1])) + [0]:
                for i in range(axes[h][0]):
                    a, b = turn(h, i, hop)
                    landed = core_in.at[(k * nx + a) * ny + b, :, span(h, width)]
                    remote(landed, landed, rcore_sem, (k, a, b, h), device(other=1)).wait_recv()
                    add_into(slot(k, a, b), h, [landed])
                    if hop > 0:
                        send(first_copy(k, h, i, hop))

    def back_b(k):
        for h in range(2):
            for i in list(range(1, axes[h][0])) + [0]:
                a, b = turn(h, i, 0)
                landed = []
                for hop in range(1, axes[h][1]):
                    first_copy(k, h, i, hop).wait_recv()
                    landed.append(first_in.at[h, (k * most + i) * most + hop])
                add_into(slot(k, a, b), h, landed)
                if i > 0:
                    send(second_copy(k, h, i))

    def back_c(k):
        for h in range(2):
            landed = []
            for i in range(1, axes[h][0]):
                second_copy(k, h, i).wait_recv()
                landed.append(second_in.at[h, k * most + i])
            add_into(slot(k, 0, 0), h, landed)
            if k > 0:
                send(plane_copy(k, h))

    order = list(range(1, nz)) + [0]
    for step in range(nz + 2):
        if step < nz:
            back_a(order[step])
        if 0 <= step - 1 < nz:
            back_b(order[step - 1])
        if 0 <= step - 2 < nz:
            back_c(order[step - 2])
    for h in range(2):
        value = rows_out[slot(0, 0, 0), :, span(h, width)].astype(jnp.float32)
        for k in range(1, nz):
            plane_copy(k, h).wait_recv()
            value = value + plane_in[k, :, span(h, width)].astype(jnp.float32)
        out_ref[:, span(h, width)] = value.astype(jnp.bfloat16)
    for copy in sent:
        copy.wait_send()


def expert_layer(moe_input, expert_ids, gate_weights, expert_gate, expert_up, expert_down):
    ranks_dp, ranks_ep = lax.axis_size("dp"), lax.axis_size("ep")
    nx = ranks_ep if ranks_dp % (2 * ranks_ep) == 0 else 1
    dims = (ranks_dp // (2 * nx), nx, ranks_ep)
    nz, ny, most = dims[0], dims[2], max(nx, ranks_ep)
    rows, width = moe_input.shape
    ranks_all = ranks_dp * ranks_ep
    half = width // 2
    named = expert_ids[:, :, None] == jnp.arange(ranks_dp, dtype=jnp.int32)[None, None, :]
    table = jnp.sum(jnp.where(named, gate_weights[:, :, None], 0.0), axis=1)
    high = lax.reduce_precision(table, 8, 7)
    middle = lax.reduce_precision(table - high, 8, 7)
    low = table - high - middle
    pad = -3 * ranks_dp % 128
    coded = jnp.pad(jnp.concatenate([high, middle, low], axis=1), ((0, 0), (0, pad)))
    block = jnp.concatenate([moe_input, coded.astype(jnp.bfloat16)], axis=1)
    full = block.shape[1]
    units = expert_gate.shape[2]
    dma = pltpu.SemaphoreType.DMA
    bf16, f32 = jnp.bfloat16, jnp.float32
    anywhere = pl.BlockSpec(memory_space=pl.ANY)
    return pl.pallas_call(
        functools.partial(expert_kernel, dims, ranks_dp),
        out_shape=jax.ShapeDtypeStruct((rows, width), bf16),
        in_specs=[anywhere] * 4,
        out_specs=pl.BlockSpec(memory_space=pltpu.VMEM),
        scratch_shapes=[
            pltpu.VMEM((ranks_all, rows, full), bf16),
            pltpu.VMEM((ranks_all, rows, width), bf16),
            pltpu.VMEM((width, units), bf16),
            pltpu.VMEM((width, units), bf16),
            pltpu.VMEM((units, width), bf16),
            pltpu.VMEM((2, ranks_all * rows, units), f32),
            pltpu.VMEM((ranks_all * rows, 1), f32),
            pltpu.VMEM((ranks_all // 2, rows, width), bf16),
            pltpu.VMEM((2, nz * most * most, rows, half), bf16),
            pltpu.VMEM((2, nz * most, rows, half), bf16),
            pltpu.VMEM((nz, rows, width), bf16),
            dma((4,)),
            dma((2, nz, 2)),
            dma((2, nz, 2, 2, most)),
            dma((2, nz, 2, most, most)),
            dma((2, nz, nx, ny, 2)),
            dma((2, nz, nx, ny, 2)),
            dma((2, nz, 2, most, most)),
            dma((2, nz, 2, most)),
            dma((2, nz, 2)),
        ],
        compiler_params=pltpu.CompilerParams(
            collective_id=0, has_side_effects=True, vmem_limit_bytes=63 * 1024 * 1024
        ),
    )(block, expert_gate, expert_up, expert_down)


def per_device(
    query_rows,
    cache_latent,
    lengths,
    moe_input,
    expert_ids,
    gate_weights,
    expert_gate,
    expert_up,
    expert_down,
):
    ranks_dp = lax.axis_size("dp")
    ranks_ep = lax.axis_size("ep")
    here_dp = lax.axis_index("dp")
    here_ep = lax.axis_index("ep")
    own_rank = here_dp * ranks_ep + here_ep
    own_length = lengths[own_rank]
    query_row = query_rows[0]
    score_top, weight_sum, mixed_values = local_attend(query_row, cache_latent, own_length)
    attn_out = (mixed_values / weight_sum[:, None]).astype(jnp.bfloat16)[None]
    moe_out = expert_layer(
        moe_input, expert_ids, gate_weights, expert_gate, expert_up, expert_down
    )
    return (attn_out, moe_out)


def solution(mesh):
    placed = (
        P(("dp", "ep"), None, None),
        P(("dp", "ep"), None),
        P(),
        P(("dp", "ep"), None),
        P(("dp", "ep"), None),
        P(("dp", "ep"), None),
        P("dp", None, "ep"),
        P("dp", None, "ep"),
        P("dp", "ep", None),
    )
    return jax.shard_map(
        per_device,
        mesh=mesh,
        in_specs=placed,
        out_specs=(P(("dp", "ep"), None, None), P(("dp", "ep"), None)),
        check_vma=False,
    )
```

```python
import functools

import jax
import jax.numpy as jnp
from jax import lax
from jax.experimental import pallas as pl
from jax.experimental.pallas import tpu as pltpu
from jax.sharding import PartitionSpec as P

WIDTH = 7168
LATENT = 512

qk_scale = 192.0 ** (-0.5)
far_low = -1e30
attend_rows = 512


def joint_kernel(
    dims, expert_total, length_ref, query_ref, cache_hbm, x_ref, gate_hbm, up_hbm, down_hbm,
    attn_ref, out_ref, cache_buf, mixed_buf, sum_buf, top_buf,
    rows_in, rows_out, gate_buf, up_buf, down_buf, act_buf, weight_buf,
    core_in, first_in, second_in, plane_in,
    load_sem, z_sem, near_sem, far_sem, core_sem, rcore_sem, rfirst_sem, rsecond_sem, rplane_sem,
):
    nz, nx, ny = dims
    width = down_buf.shape[1]
    half = width // 2
    full = rows_in.shape[2]
    dp, y = lax.axis_index("dp"), lax.axis_index("ep")
    core, x, z = dp % 2, (dp // 2) % nx, dp // (2 * nx)

    def slot(k, a, b, other=0):
        c = 1 - core if other else core
        return ((((z + k) % nz) * nx + (x + a) % nx) * 2 + c) * ny + (y + b) % ny

    def device(k=0, a=0, b=0, other=0):
        c = 1 - core if other else core
        return ((((z + k) % nz) * nx + (x + a) % nx) * 2 + c, (y + b) % ny)

    def span(h, top):
        return pl.ds(0, half) if h == 0 else pl.ds(half, top - half)

    cache_load = pltpu.make_async_copy(cache_hbm, cache_buf, load_sem.at[4])
    loads = [
        pltpu.make_async_copy(gate_hbm.at[0], gate_buf, load_sem.at[1]),
        pltpu.make_async_copy(up_hbm.at[0], up_buf, load_sem.at[2]),
        pltpu.make_async_copy(down_hbm.at[0], down_buf, load_sem.at[3]),
    ]
    mine = pltpu.make_async_copy(x_ref, rows_in.at[slot(0, 0, 0)], load_sem.at[0])
    mine.start()
    barrier = pltpu.get_barrier_semaphore()
    partners = [device(other=1)]
    partners += [device(k=k) for k in range(1, nz)]
    partners += [device(a=a) for a in range(1, nx)]
    partners += [device(b=b) for b in range(1, ny)]
    for partner in partners:
        pl.semaphore_signal(barrier, inc=1, device_id=partner, device_id_type=pl.DeviceIdType.MESH)
    cache_load.start()
    for load in loads:
        load.start()
    pl.semaphore_wait(barrier, len(partners))
    mine.wait()

    def remote(src, dst, sems, index, target):
        return pltpu.make_async_remote_copy(
            src_ref=src,
            dst_ref=dst,
            send_sem=sems.at[(0,) + index],
            recv_sem=sems.at[(1,) + index],
            device_id=target,
            device_id_type=pl.DeviceIdType.MESH,
        )

    sent = []

    def send(copy):
        copy.start()
        sent.append(copy)

    def block_copy(source, h, sems, index, target):
        part = rows_in.at[source, :, span(h, full)]
        return remote(part, part, sems, index, target)

    def to_core(k, a, b, h):
        send(block_copy(slot(-k, -a, -b), h, core_sem, (k, a, b, h), device(other=1)))

    for k in range(1, nz):
        for h in range(2):
            send(block_copy(slot(0, 0, 0), h, z_sem, (k, h), device(k=k)))

    axes = {0: (nx, ny), 1: (ny, nx)}

    def turn(h, first, second):
        return (first, second) if h == 0 else (second, first)

    def near(k, h, way, hop):
        a, b = turn(h, hop, 0) if way == 0 else turn(h, 0, hop)
        return block_copy(slot(-k, 0, 0), h, near_sem, (k, h, way, hop), device(a=a, b=b))

    def far(k, h, i, hop):
        a, b = turn(h, 0, hop)
        sa, sb = turn(h, i, 0)
        return block_copy(slot(-k, -sa, -sb), h, far_sem, (k, h, i, hop), device(a=a, b=b))

    def stage_a(k):
        for h in range(2):
            if k > 0:
                block_copy(slot(-k, 0, 0), h, z_sem, (k, h), device(k=k)).wait_recv()
            for way in range(2):
                for hop in range(1, axes[h][way]):
                    send(near(k, h, way, hop))
            to_core(k, 0, 0, h)

    def arrived(k, a, b, h, sems, index):
        block_copy(slot(-k, -a, -b), h, sems, index, device(other=1)).wait_recv()

    def stage_b(k):
        for h in range(2):
            for i in range(1, axes[h][0]):
                a, b = turn(h, i, 0)
                arrived(k, a, b, h, near_sem, (k, h, 0, i))
                for hop in range(1, axes[h][1]):
                    send(far(k, h, i, hop))
                to_core(k, a, b, h)

    def stage_c(k):
        for h in range(2):
            for hop in range(1, axes[h][1]):
                a, b = turn(h, 0, hop)
                arrived(k, a, b, h, near_sem, (k, h, 1, hop))
                to_core(k, a, b, h)
                for i in range(1, axes[h][0]):
                    a, b = turn(h, i, hop)
                    arrived(k, a, b, h, far_sem, (k, h, i, hop))
                    to_core(k, a, b, h)

    blocks = cache_buf.shape[1] // attend_rows
    length = length_ref[dp * ny + y]
    query = query_ref[0].T

    def attend_block(block):
        keys = cache_buf[:, block * attend_rows : (block + 1) * attend_rows]
        place = lax.broadcasted_iota(jnp.int32, (1, attend_rows), 1) + block * attend_rows
        scores = qk_scale * jnp.dot(query, keys, preferred_element_type=jnp.float32)
        scores = jnp.where(place < length, scores, far_low)
        top = jnp.max(scores, axis=1, keepdims=True)
        if block > 0:
            top = jnp.maximum(top_buf[...], top)
        exponent = jnp.where(place < length, jnp.exp(scores - top), 0.0)
        weight = jnp.sum(exponent, axis=1, keepdims=True)
        mixed = lax.dot_general(
            exponent.astype(jnp.bfloat16),
            keys[:LATENT],
            (((1,), (1,)), ((), ())),
            preferred_element_type=jnp.float32,
        )
        if block > 0:
            scale = jnp.exp(top_buf[...] - top)
            weight = weight + sum_buf[...] * scale
            mixed = mixed + mixed_buf[...] * scale
        top_buf[...] = top
        sum_buf[...] = weight
        mixed_buf[...] = mixed

    units = [functools.partial(attend_block, block) for block in range(blocks)][::-1]

    def attend(number):
        for _ in range(min(number, len(units))):
            units.pop()()

    for step in range(nz + 2):
        if step < nz:
            stage_a(step)
        if step == 0:
            cache_load.wait()
            attend(2)
        else:
            attend(1)
        if 0 <= step - 1 < nz:
            stage_b(step - 1)
            attend(1)
        if 0 <= step - 2 < nz:
            stage_c(step - 2)
            attend(1)
    attend(len(units))
    attn_ref[0] = mixed_buf[...] / sum_buf[...]
    for k in range(nz):
        for a in range(nx):
            for b in range(ny):
                for h in range(2):
                    block_copy(
                        slot(-k, -a, -b, 1), h, core_sem, (k, a, b, h), device(other=1)
                    ).wait_recv()
    loads[0].wait()
    loads[1].wait()
    count, rows = rows_in.shape[0], rows_in.shape[1]
    total = count * rows
    hidden_units = gate_buf.shape[1]
    depth = 1024
    act_buf[...] = jnp.zeros_like(act_buf)

    @pl.loop(0, width // depth)
    def _(step):
        cols = pl.ds(pl.multiple_of(step * depth, depth), depth)
        lhs = rows_in[:, :, cols].astype(jnp.float32).reshape(total, depth).astype(jnp.bfloat16)
        act_buf[0] += jnp.dot(lhs, gate_buf[cols, :], preferred_element_type=jnp.float32)
        act_buf[1] += jnp.dot(lhs, up_buf[cols, :], preferred_element_type=jnp.float32)

    coded = rows_in[:, :, width:].astype(jnp.float32).reshape(total, full - width)
    lane = lax.broadcasted_iota(jnp.int32, coded.shape, 1)
    chosen = (lane == dp) | (lane == dp + expert_total) | (lane == dp + 2 * expert_total)
    weight_buf[...] = jnp.sum(jnp.where(chosen, coded, 0.0), axis=1, keepdims=True)
    gate_act = act_buf[0]
    hidden = (gate_act / (1.0 + jnp.exp(-gate_act)) * act_buf[1]).astype(jnp.bfloat16)
    loads[2].wait()
    piece = 512
    for h in range(2):

        @pl.loop(0, half // piece)
        def _(step, h=h):
            cols = pl.ds(pl.multiple_of(h * half + step * piece, piece), piece)
            product = jnp.dot(hidden, down_buf[:, cols], preferred_element_type=jnp.float32)
            product = product * weight_buf[...]
            rows_out[:, :, cols] = product.reshape(count, rows, piece).astype(jnp.bfloat16)

        for k in list(range(1, nz)) + [0]:
            for a in range(nx):
                for b in range(ny):
                    send(
                        remote(
                            rows_out.at[slot(k, a, b, 1), :, span(h, width)],
                            core_in.at[(k * nx + a) * ny + b, :, span(h, width)],
                            rcore_sem,
                            (k, a, b, h),
                            device(other=1),
                        )
                    )

    def add_into(target, h, landed):
        value = rows_out[target, :, span(h, width)].astype(jnp.float32)
        for piece_ref in landed:
            value = value + piece_ref[...].astype(jnp.float32)
        rows_out[target, :, span(h, width)] = value.astype(jnp.bfloat16)

    most = max(nx, ny)

    def first_copy(k, h, i, hop):
        a, b = turn(h, i, hop)
        da, db = turn(h, 0, hop)
        return remote(
            rows_out.at[slot(k, a, b), :, span(h, width)],
            first_in.at[h, (k * most + i) * (most - 1) + hop - 1],
            rfirst_sem, (k, h, i, hop), device(a=da, b=db),
        )

    def second_copy(k, h, i):
        a, b = turn(h, i, 0)
        return remote(
            rows_out.at[slot(k, a, b), :, span(h, width)],
            second_in.at[h, k * (most - 1) + i - 1],
            rsecond_sem, (k, h, i), device(a=a, b=b),
        )

    def plane_copy(k, h):
        return remote(
            rows_out.at[slot(k, 0, 0), :, span(h, width)],
            plane_in.at[k - 1, :, span(h, width)],
            rplane_sem, (k, h), device(k=k),
        )

    def back_a(k):
        for h in range(2):
            for hop in list(range(1, axes[h][1])) + [0]:
                for i in range(axes[h][0]):
                    a, b = turn(h, i, hop)
                    landed = core_in.at[(k * nx + a) * ny + b, :, span(h, width)]
                    remote(landed, landed, rcore_sem, (k, a, b, h), device(other=1)).wait_recv()
                    add_into(slot(k, a, b), h, [landed])
                    if hop > 0:
                        send(first_copy(k, h, i, hop))

    def back_b(k):
        for h in range(2):
            for i in list(range(1, axes[h][0])) + [0]:
                a, b = turn(h, i, 0)
                landed = []
                for hop in range(1, axes[h][1]):
                    first_copy(k, h, i, hop).wait_recv()
                    landed.append(first_in.at[h, (k * most + i) * (most - 1) + hop - 1])
                add_into(slot(k, a, b), h, landed)
                if i > 0:
                    send(second_copy(k, h, i))

    def back_c(k):
        for h in range(2):
            landed = []
            for i in range(1, axes[h][0]):
                second_copy(k, h, i).wait_recv()
                landed.append(second_in.at[h, k * (most - 1) + i - 1])
            add_into(slot(k, 0, 0), h, landed)
            if k > 0:
                send(plane_copy(k, h))

    order = list(range(1, nz)) + [0]
    for step in range(nz + 2):
        if step < nz:
            back_a(order[step])
        if 0 <= step - 1 < nz:
            back_b(order[step - 1])
        if 0 <= step - 2 < nz:
            back_c(order[step - 2])
    for h in range(2):
        value = rows_out[slot(0, 0, 0), :, span(h, width)].astype(jnp.float32)
        for k in range(1, nz):
            plane_copy(k, h).wait_recv()
            value = value + plane_in[k - 1, :, span(h, width)].astype(jnp.float32)
        out_ref[:, span(h, width)] = value
    for copy in sent:
        copy.wait_send()


def both_layers(lengths, query_rows, cache_latent, moe_input, expert_ids, gate_weights, expert_gate, expert_up, expert_down):
    ranks_dp, ranks_ep = lax.axis_size("dp"), lax.axis_size("ep")
    nx = ranks_ep if ranks_dp % (2 * ranks_ep) == 0 else 1
    dims = (ranks_dp // (2 * nx), nx, ranks_ep)
    nz, ny, most = dims[0], dims[2], max(nx, ranks_ep)
    rows, width = moe_input.shape
    ranks_all = ranks_dp * ranks_ep
    half = width // 2
    named = expert_ids[:, :, None] == jnp.arange(ranks_dp, dtype=jnp.int32)[None, None, :]
    table = jnp.sum(jnp.where(named, gate_weights[:, :, None], 0.0), axis=1)
    high = lax.reduce_precision(table, 8, 7)
    middle = lax.reduce_precision(table - high, 8, 7)
    low = table - high - middle
    pad = -3 * ranks_dp % 128
    coded = jnp.pad(jnp.concatenate([high, middle, low], axis=1), ((0, 0), (0, pad)))
    block = jnp.concatenate([moe_input, coded.astype(jnp.bfloat16)], axis=1)
    full = block.shape[1]
    units = expert_gate.shape[2]
    dma = pltpu.SemaphoreType.DMA
    bf16, f32 = jnp.bfloat16, jnp.float32
    anywhere = pl.BlockSpec(memory_space=pl.ANY)
    heads = query_rows.shape[2]
    return pl.pallas_call(
        functools.partial(joint_kernel, dims, ranks_dp),
        out_shape=(
            jax.ShapeDtypeStruct((1, heads, LATENT), f32),
            jax.ShapeDtypeStruct((rows, width), f32),
        ),
        in_specs=[
            pl.BlockSpec(memory_space=pltpu.SMEM),
            pl.BlockSpec(memory_space=pltpu.VMEM),
        ]
        + [anywhere] * 5,
        out_specs=(pl.BlockSpec(memory_space=pltpu.VMEM),) * 2,
        scratch_shapes=[
            pltpu.VMEM(cache_latent.shape, bf16),
            pltpu.VMEM((heads, LATENT), f32),
            pltpu.VMEM((heads, 1), f32),
            pltpu.VMEM((heads, 1), f32),
            pltpu.VMEM((ranks_all, rows, full), bf16),
            pltpu.VMEM((ranks_all, rows, width), bf16),
            pltpu.VMEM((width, units), bf16),
            pltpu.VMEM((width, units), bf16),
            pltpu.VMEM((units, width), bf16),
            pltpu.VMEM((2, ranks_all * rows, units), f32),
            pltpu.VMEM((ranks_all * rows, 1), f32),
            pltpu.VMEM((ranks_all // 2, rows, width), bf16),
            pltpu.VMEM((2, nz * most * max(most - 1, 1), rows, half), bf16),
            pltpu.VMEM((2, nz * max(most - 1, 1), rows, half), bf16),
            pltpu.VMEM((max(nz - 1, 1), rows, width), bf16),
            dma((5,)),
            dma((2, nz, 2)),
            dma((2, nz, 2, 2, most)),
            dma((2, nz, 2, most, most)),
            dma((2, nz, nx, ny, 2)),
            dma((2, nz, nx, ny, 2)),
            dma((2, nz, 2, most, most)),
            dma((2, nz, 2, most)),
            dma((2, nz, 2)),
        ],
        compiler_params=pltpu.CompilerParams(
            collective_id=0, has_side_effects=True, vmem_limit_bytes=67043328
        ),
    )(lengths, query_rows, cache_latent, block, expert_gate, expert_up, expert_down)


def per_device(
    query_rows,
    cache_latent,
    lengths,
    moe_input,
    expert_ids,
    gate_weights,
    expert_gate,
    expert_up,
    expert_down,
):
    attn_out, moe_out = both_layers(
        lengths, jnp.swapaxes(query_rows, 1, 2), cache_latent.T, moe_input, expert_ids,
        gate_weights, expert_gate, expert_up, expert_down,
    )
    return attn_out.astype(jnp.bfloat16), moe_out.astype(jnp.bfloat16)


def solution(mesh):
    placed = (
        P(("dp", "ep"), None, None),
        P(("dp", "ep"), None),
        P(),
        P(("dp", "ep"), None),
        P(("dp", "ep"), None),
        P(("dp", "ep"), None),
        P("dp", None, "ep"),
        P("dp", None, "ep"),
        P("dp", "ep", None),
    )
    return jax.shard_map(
        per_device,
        mesh=mesh,
        in_specs=placed,
        out_specs=(P(("dp", "ep"), None, None), P(("dp", "ep"), None)),
        check_vma=False,
    )
```
